128 devices in a mesh: freq: 4 (over z), tile: 32 (over x, y, core).
Axes of the slice: x: 4, y: 4, z: 4, core: 2. Of those that a mesh axis runs over, the one named last changes fastest.
Arguments:
- model_freq: bfloat16 [8, 16384, 384], P('freq', 'tile'), may hold values from -6 to 6
- recorded: bfloat16 [8, 16384, 384], P('freq', 'tile'), may hold values from -6 to 6
- v_factor: bfloat16 [8, 32, 32, 2, 64, 512], P('freq', 'tile'), may hold values from -0.25 to 0.25
- u_factor: bfloat16 [8, 32, 32, 2, 64, 512], P('freq', 'tile'), may hold values from -0.125 to 0.125
- tile_rank: int32 [8, 32, 32], P('freq', 'tile'), may hold values from 16 to 64
- tile_rows: int32 [32, 32], P('tile'), may hold values from 0 to 31, each once within a row
- omega: float32 [8], P('freq'), may hold values from 0.3 to 2.9
Outputs:
- lag_gradient: float32 [8, 16384, 192], P('freq', 'tile')
The draws below stay inside these ranges and needn't reach their ends.
Inputs may be any that keep to these rules, and one draw needn't show every extreme that they name: Each row of tile_rows is a permutation of 0 to 31.
All inputs are finite; a program needn't handle non-finite values.
Results may differ from the reference program's by a relative error of at most 0.0037.
Values may be sent and summed in bfloat16 or wider, within the bound.
No kernel may reach another device: no remote copies, remote signals or barrier semaphores. Data moves between devices by JAX's collectives and lax.ppermute only.
A program may use at most 128 MiB of HBM per device.

```python
import jax
import jax.numpy as jnp
from jax import lax

TB = 32
TS = 512
RANK = 64
SOURCES = 192
ORDER = 16384
FREQS = 8
LAGS = 8


def touch_ends(drawn, key, low, high):
    spot = [jax.random.randint(jax.random.fold_in(key, axis), (), 0, length) for axis, length in enumerate(drawn.shape)]
    longest = drawn.shape.index(max(drawn.shape))
    beside = spot[:longest] + [(spot[longest] + 1) % drawn.shape[longest]] + spot[longest + 1:]
    return drawn.at[tuple(spot)].set(low).at[tuple(beside)].set(high)


def block_scale(key, shape, cuts, low, high):
    level = 1.0
    for position, parts in cuts:
        heights = jax.random.uniform(jax.random.fold_in(jax.random.fold_in(key, 6), position), (parts,), jnp.float32, low / len(cuts), high / len(cuts))
        level = level * jnp.repeat(jnp.exp(heights), shape[position] // parts).reshape((-1,) + (1,) * (len(shape) - 1 - position))
    return level


def bell_draw(rng, shape, scale, reach, shards=(), kind=jnp.bfloat16):
    result = scale * jax.random.normal(rng, shape, jnp.float32)
    if shards:
        result = result * block_scale(rng, shape, shards, -0.22, 0.18)
    return jnp.clip(result, -reach, reach).astype(kind)


def setup_inputs(seed: int = 0) -> dict:
    keys = jax.random.split(jax.random.key(seed), 8)
    model_freq = bell_draw(keys[0], (FREQS, ORDER, 2 * SOURCES), 1.0, 6.0, ((0, 4), (1, 32)))
    recorded = bell_draw(keys[1], (FREQS, ORDER, 2 * SOURCES), 1.0, 6.0, ((0, 4), (1, 32)))
    v_factor = bell_draw(keys[2], (FREQS, TB, TB, 2, RANK, TS), TS ** -0.5, 0.25, ((0, 4), (1, 32)))
    u_factor = bell_draw(keys[3], (FREQS, TB, TB, 2, RANK, TS), (TB * RANK) ** -0.5, 0.125, ((0, 4), (1, 32)))
    tile_rank = touch_ends(jax.random.randint(keys[4], (FREQS, TB, TB), RANK // 4, RANK + 1), jax.random.fold_in(keys[4], 1), RANK // 4, RANK).astype(jnp.int32)
    tile_rows = jax.vmap(lambda own: jax.random.permutation(own, TB))(jax.random.split(keys[5], TB)).reshape((TB, TB)).astype(jnp.int32)
    omega = jnp.clip(0.3 + 2.6000001 * jax.random.uniform(keys[6], (FREQS,), jnp.float32) ** block_scale(keys[6], (FREQS,), ((0, 4),), -0.2, 0.2), 0.3, 2.9)
    return {"model_freq": model_freq, "recorded": recorded, "v_factor": v_factor, "u_factor": u_factor, "tile_rank": tile_rank, "tile_rows": tile_rows, "omega": omega}


def reference(model_freq, recorded, v_factor, u_factor, tile_rank, tile_rows, omega):
    half = SOURCES
    select = (tile_rows[:, :, None] == jnp.arange(TB, dtype=jnp.int32)[None, None, :]).astype(jnp.float32)

    def one_freq(item):
        model_one, data_one, v_one, u_one, rank_one = item
        blocks = model_one.reshape(TB, TS, 2 * half).astype(jnp.float32)
        v_real = v_one[:, :, 0].astype(jnp.float32)
        v_imag = v_one[:, :, 1].astype(jnp.float32)
        first = jnp.einsum("jkrt,jts->jkrs", v_real, blocks)
        second = jnp.einsum("jkrt,jts->jkrs", v_imag, blocks)
        coeff = jnp.concatenate([first[..., :half] - second[..., half:], first[..., half:] + second[..., :half]], -1)
        keep = (jnp.arange(RANK, dtype=jnp.int32)[None, None, :] < rank_one[:, :, None]).astype(jnp.float32)[..., None]
        coeff = (coeff * keep).astype(jnp.bfloat16)
        natural = jnp.einsum("jki,jkrs->ijrs", select, coeff.astype(jnp.float32))
        u_real = u_one[:, :, 0].astype(jnp.float32)
        u_imag = u_one[:, :, 1].astype(jnp.float32)
        upper = jnp.einsum("ijrt,ijrs->its", u_real, natural)
        lower = jnp.einsum("ijrt,ijrs->its", u_imag, natural)
        forward = jnp.concatenate([upper[..., :half] - lower[..., half:], upper[..., half:] + lower[..., :half]], -1)
        resid = (forward - data_one.reshape(TB, TS, 2 * half).astype(jnp.float32)).astype(jnp.bfloat16)
        resid = resid.astype(jnp.float32)
        back_re = jnp.einsum("ijrt,its->ijrs", u_real, resid)
        back_im = jnp.einsum("ijrt,its->ijrs", u_imag, resid)
        back = jnp.concatenate([back_re[..., :half] + back_im[..., half:], back_re[..., half:] - back_im[..., :half]], -1)
        back = back.astype(jnp.bfloat16)
        slotted = jnp.einsum("jki,ijrs->jkrs", select, back.astype(jnp.float32)) * keep
        grad_a = jnp.einsum("jkrt,jkrs->jts", v_real, slotted)
        grad_b = jnp.einsum("jkrt,jkrs->jts", v_imag, slotted)
        grad = jnp.concatenate([grad_a[..., :half] + grad_b[..., half:], grad_a[..., half:] - grad_b[..., :half]], -1)
        return grad.reshape(TB * TS, 2 * half)

    grads = lax.map(one_freq, (model_freq, recorded, v_factor, u_factor, tile_rank))
    lag_axis = jnp.arange(LAGS, dtype=jnp.float32)
    phase = lag_axis[:, None] * omega[None, :]
    cosine = jnp.cos(phase)
    sine = jnp.sin(phase)
    total = jnp.einsum("lf,fns->lns", cosine, grads[..., :half], precision=lax.Precision.HIGHEST)
    total = total - jnp.einsum("lf,fns->lns", sine, grads[..., half:], precision=lax.Precision.HIGHEST)
    return total * (2.0 / FREQS)
```

```python
import functools

import jax
import jax.numpy as jnp
from jax import lax
from jax.experimental import pallas as pl
from jax.experimental.pallas import tpu as pltpu
from jax.sharding import PartitionSpec as P

SOURCES = 192
LAG_DEV = 2
CHUNKS = (96, 96)
PER_STEP = 8
VMEM_LIMIT = 48 * 1024 * 1024
NT = (((1,), (1,)), ((), ()))


def lane_sign(rank):
    lane = lax.broadcasted_iota(jnp.int32, (1, 2 * rank), 1)
    return jnp.where(lane < rank, 1.0, -1.0).astype(jnp.float32)


def rank_lane(rank):
    lane = lax.broadcasted_iota(jnp.int32, (1, 2 * rank), 1)
    return jnp.where(lane < rank, lane, lane - rank)


def coeff_kernel(ranks, rows, x_ref, v_ref, out_ref, x_t, *, start, count, rank):
    f = pl.program_id(0)
    step = pl.program_id(1)
    wide = 2 * rank
    half = x_ref.shape[2] // 2

    @pl.when(step == 0)
    def _():
        turned = x_ref[0].T
        x_t[:count] = turned[start:start + count]
        x_t[count:] = turned[half + start:half + start + count]

    product = lax.dot_general(x_t[...], v_ref[0], NT, preferred_element_type=jnp.float32)
    sign = -lane_sign(rank)
    index = rank_lane(rank)
    for t in range(PER_STEP):
        slot = step * PER_STEP + t
        real = product[:count, t * wide:(t + 1) * wide]
        imag = product[count:, t * wide:(t + 1) * wide]
        value = real + sign * pltpu.roll(imag, rank, 1)
        value = jnp.where(index < ranks[f, slot], value, 0.0)
        out_ref[rows[0, slot], 0] = value.astype(out_ref.dtype)


def resid_kernel(c_ref, u_ref, rec_ref, out_ref, left, total, *, start, count, rank, tiles):
    wide = 2 * rank
    half = rec_ref.shape[2] // 2
    sign = lane_sign(rank)
    groups = tiles // PER_STEP
    span = PER_STEP * wide

    total[...] = jnp.zeros_like(total)

    def gather(g, carry):
        for t in range(PER_STEP):
            tile = c_ref[g * PER_STEP + t, 0].astype(jnp.float32)
            left[:count, t * wide:(t + 1) * wide] = (tile * sign).astype(left.dtype)
            left[count:, t * wide:(t + 1) * wide] = pltpu.roll(tile, rank, 1).astype(left.dtype)
        total[...] += jnp.dot(
            left[...], u_ref[0, pl.ds(pl.multiple_of(g * span, span), span)],
            preferred_element_type=jnp.float32,
        )
        return carry

    lax.fori_loop(0, groups, gather, 0)
    turned = rec_ref[0].T.astype(jnp.float32)
    observed = jnp.concatenate(
        [turned[start:start + count], turned[half + start:half + start + count]], 0
    )
    resid = (total[...] - observed).astype(jnp.bfloat16)

    def spread(g, carry):
        product = lax.dot_general(
            resid, u_ref[0, pl.ds(pl.multiple_of(g * span, span), span)], NT,
            preferred_element_type=jnp.float32,
        )
        for t in range(PER_STEP):
            real = product[:count, t * wide:(t + 1) * wide]
            imag = product[count:, t * wide:(t + 1) * wide]
            value = sign * real + pltpu.roll(imag, rank, 1)
            out_ref[g * PER_STEP + t, 0] = value.astype(out_ref.dtype)
        return carry

    lax.fori_loop(0, groups, spread, 0)


def grad_kernel(ranks, rows, cosine, sine, b_ref, v_ref, out_ref, left, total, lags,
                *, count, rank, tiles):
    f = pl.program_id(0)
    wide = 2 * rank
    sign = lane_sign(rank)
    index = rank_lane(rank)
    groups = tiles // PER_STEP
    span = PER_STEP * wide
    lag_total = out_ref.shape[0] * out_ref.shape[1]

    total[...] = jnp.zeros_like(total)

    def gather(g, carry):
        for t in range(PER_STEP):
            slot = g * PER_STEP + t
            tile = b_ref[rows[0, slot], 0].astype(jnp.float32)
            tile = jnp.where(index < ranks[f, slot], tile, 0.0)
            left[:count, t * wide:(t + 1) * wide] = tile.astype(left.dtype)
            left[count:, t * wide:(t + 1) * wide] = (
                sign * pltpu.roll(tile, rank, 1)
            ).astype(left.dtype)
        total[...] += jnp.dot(
            left[...], v_ref[0, pl.ds(pl.multiple_of(g * span, span), span)],
            preferred_element_type=jnp.float32,
        )
        return carry

    lax.fori_loop(0, groups, gather, 0)

    for lag in range(lag_total):
        share = total[:count] * cosine[lag, f] - total[count:] * sine[lag, f]

        @pl.when(f == 0)
        def _():
            lags[lag] = share

        @pl.when(f == pl.num_programs(0) - 1)
        def _():
            whole = lags[lag] + share
            out_ref[lag // LAG_DEV, lag % LAG_DEV] = whole.astype(out_ref.dtype)


def finish_kernel(*refs):
    out_ref = refs[-1]
    parts = []
    for ref in refs[:-1]:
        parts.append(
            (ref[0, 0].astype(jnp.float32) + ref[1, 0].astype(jnp.float32))
            + (ref[2, 0].astype(jnp.float32) + ref[3, 0].astype(jnp.float32))
        )
    out_ref[0] = jnp.concatenate(parts, 0)


def per_device(model_freq, recorded, v_factor, u_factor, tile_rank, tile_rows, omega):
    freqs = v_factor.shape[0]
    tiles = v_factor.shape[2]
    rank = v_factor.shape[4]
    width = v_factor.shape[5]
    columns = model_freq.shape[2]
    wide = 2 * rank
    depth = tiles * wide
    steps = tiles // PER_STEP
    groups = lax.axis_size("freq")
    freq_total = freqs * groups
    lag_total = LAG_DEV * groups
    v_flat = v_factor.reshape(freqs, depth, width)
    u_flat = u_factor.reshape(freqs, depth, width)
    ranks = tile_rank.reshape(freqs, tiles)
    phase = jnp.arange(lag_total, dtype=jnp.float32)[:, None] * omega[None, :]
    cosine = jnp.cos(phase) * (2.0 / freq_total)
    sine = jnp.sin(phase) * (2.0 / freq_total)

    def params():
        return pltpu.CompilerParams(
            dimension_semantics=None, vmem_limit_bytes=VMEM_LIMIT
        )

    def cost(count, factors):
        return pl.CostEstimate(
            flops=factors * freqs * 2 * 2 * count * depth * width,
            bytes_accessed=freqs * depth * width * 2 + 4 * freqs * tiles * count * wide,
            transcendentals=0,
        )

    smem = pl.BlockSpec(memory_space=pltpu.SMEM)

    def coeff(start, count):
        return pl.pallas_call(
            functools.partial(coeff_kernel, start=start, count=count, rank=rank),
            grid=(freqs, steps),
            in_specs=[
                smem,
                smem,
                pl.BlockSpec((1, width, columns), lambda f, s: (f, 0, 0)),
                pl.BlockSpec((1, depth // steps, width), lambda f, s: (f, s, 0)),
            ],
            out_specs=pl.BlockSpec((tiles, 1, count, wide), lambda f, s: (0, f, 0, 0)),
            out_shape=jax.ShapeDtypeStruct((tiles, freqs, count, wide), jnp.bfloat16),
            scratch_shapes=[pltpu.VMEM((2 * count, width), jnp.bfloat16)],
            compiler_params=params(),
            cost_estimate=cost(count, 1),
            name="coeff",
        )(ranks, tile_rows, model_freq, v_flat)

    def resid(arrived, start, count):
        return pl.pallas_call(
            functools.partial(resid_kernel, start=start, count=count, rank=rank, tiles=tiles),
            grid=(freqs,),
            in_specs=[
                pl.BlockSpec((tiles, 1, count, wide), lambda f: (0, f, 0, 0)),
                pl.BlockSpec((1, depth, width), lambda f: (f, 0, 0)),
                pl.BlockSpec((1, width, columns), lambda f: (f, 0, 0)),
            ],
            out_specs=pl.BlockSpec((tiles, 1, count, wide), lambda f: (0, f, 0, 0)),
            out_shape=jax.ShapeDtypeStruct((tiles, freqs, count, wide), jnp.bfloat16),
            scratch_shapes=[
                pltpu.VMEM((2 * count, PER_STEP * wide), jnp.bfloat16),
                pltpu.VMEM((2 * count, width), jnp.float32),
            ],
            compiler_params=params(),
            cost_estimate=cost(count, 2),
            name="resid",
        )(arrived, u_flat, recorded)

    def grad(returned, count):
        return pl.pallas_call(
            functools.partial(grad_kernel, count=count, rank=rank, tiles=tiles),
            grid=(freqs,),
            in_specs=[
                smem,
                smem,
                smem,
                smem,
                pl.BlockSpec((tiles, 1, count, wide), lambda f: (0, f, 0, 0)),
                pl.BlockSpec((1, depth, width), lambda f: (f, 0, 0)),
            ],
            out_specs=pl.BlockSpec((groups, LAG_DEV, count, width), lambda f: (0, 0, 0, 0)),
            out_shape=jax.ShapeDtypeStruct((groups, LAG_DEV, count, width), jnp.bfloat16),
            scratch_shapes=[
                pltpu.VMEM((2 * count, PER_STEP * wide), jnp.bfloat16),
                pltpu.VMEM((2 * count, width), jnp.float32),
                pltpu.VMEM((lag_total, count, width), jnp.float32),
            ],
            compiler_params=params(),
            cost_estimate=cost(count, 1),
            name="grad",
        )(ranks, tile_rows, cosine, sine, returned, v_flat)

    def exchange(x, axis):
        return lax.all_to_all(x, axis, split_axis=0, concat_axis=0, tiled=True)

    starts = [sum(CHUNKS[:i]) for i in range(len(CHUNKS))]
    sent = [coeff(s, n) for s, n in zip(starts, CHUNKS)]
    arrived = [exchange(x, "tile") for x in sent]
    back = [resid(x, s, n) for x, s, n in zip(arrived, starts, CHUNKS)]
    returned = [exchange(x, "tile") for x in back]
    shares = [grad(x, n) for x, n in zip(returned, CHUNKS)]
    gathered = [exchange(x, "freq") for x in shares]
    total = pl.pallas_call(
        finish_kernel,
        grid=(LAG_DEV,),
        in_specs=[
            pl.BlockSpec((groups, 1, n, width), lambda t: (0, t, 0, 0)) for n in CHUNKS
        ],
        out_specs=pl.BlockSpec((1, SOURCES, width), lambda t: (t, 0, 0)),
        out_shape=jax.ShapeDtypeStruct((LAG_DEV, SOURCES, width), jnp.float32),
        compiler_params=params(),
        name="finish",
    )(*gathered)
    return jnp.swapaxes(total, 1, 2)


def solution(mesh):
    placed = (
        P("freq", "tile", None),
        P("freq", "tile", None),
        P("freq", "tile", None, None, None, None),
        P("freq", "tile", None, None, None, None),
        P("freq", "tile", None),
        P("tile", None),
        P("freq"),
    )
    return jax.shard_map(
        per_device, mesh=mesh, in_specs=placed, out_specs=P("freq", "tile", None), check_vma=False
    )
```

```python
import functools

import jax
import jax.numpy as jnp
from jax import lax
from jax.experimental import pallas as pl
from jax.experimental.pallas import tpu as pltpu
from jax.sharding import PartitionSpec as P

SOURCES = 192
LAG_DEV = 2
CHUNKS = (128, 64)
PER_STEP = 16
VMEM_LIMIT = 60 * 1024 * 1024
NT = (((1,), (1,)), ((), ()))


def lane_sign(rank):
    lane = lax.broadcasted_iota(jnp.int32, (1, 2 * rank), 1)
    return jnp.where(lane < rank, 1.0, -1.0).astype(jnp.float32)


def rank_lane(rank):
    lane = lax.broadcasted_iota(jnp.int32, (1, 2 * rank), 1)
    return jnp.where(lane < rank, lane, lane - rank)


def both_parts(turned, start, count):
    half = turned.shape[0] // 2
    return jnp.concatenate(
        [turned[start:start + count], turned[half + start:half + start + count]], 0
    )


def factor_copies(hbm, buf, sems):
    freqs, depth, _ = buf.shape
    groups = sems.shape[1]
    span = depth // groups

    def copy(f, g):
        at = pl.ds(pl.multiple_of(g * span, span), span)
        return pltpu.make_async_copy(hbm.at[f, at], buf.at[f, at], sems.at[f, g])

    return copy


def coeff_kernel(rank_hbm, row_hbm, x_hbm, v_hbm, out_hbm,
                 ranks, rows, x_in, x_t, v_buf, out_buf, small, x_sem, v_sem, out_sem,
                 *, start, count, rank):
    freqs, depth, width = v_buf.shape
    wide = 2 * rank
    span = PER_STEP * wide
    groups = depth // span
    factors = factor_copies(v_hbm, v_buf, v_sem)
    rank_copy = pltpu.make_async_copy(rank_hbm, ranks, small.at[0])
    row_copy = pltpu.make_async_copy(row_hbm, rows, small.at[1])

    def model(f):
        return pltpu.make_async_copy(x_hbm.at[f], x_in.at[f], x_sem.at[f])

    def result(f):
        return pltpu.make_async_copy(out_buf.at[:, f], out_hbm.at[:, f], out_sem.at[f])

    model(0).start()
    for g in range(groups):
        factors(0, g).start()
    rank_copy.start()
    row_copy.start()
    for f in range(1, freqs):
        model(f).start()
        for g in range(groups):
            factors(f, g).start()
    sign = -lane_sign(rank)
    index = rank_lane(rank)
    rank_copy.wait()
    row_copy.wait()

    def one_freq(f, carry):
        model(f).wait()
        x_t[...] = both_parts(x_in[f].T, start, count)

        def step(g, inner):
            factors(f, g).wait()
            product = lax.dot_general(
                x_t[...], v_buf[f, pl.ds(pl.multiple_of(g * span, span), span)], NT,
                preferred_element_type=jnp.float32,
            )
            for t in range(PER_STEP):
                slot = g * PER_STEP + t
                real = product[:count, t * wide:(t + 1) * wide]
                imag = product[count:, t * wide:(t + 1) * wide]
                value = real + sign * pltpu.roll(imag, rank, 1)
                value = jnp.where(index < ranks[f, 0, slot], value, 0.0)
                out_buf[rows[0, slot], f] = value.astype(out_buf.dtype)
            return inner

        lax.fori_loop(0, groups, step, 0)
        result(f).start()
        return carry

    lax.fori_loop(0, freqs, one_freq, 0)
    for f in range(freqs):
        result(f).wait()


def resid_kernel(c_hbm, u_hbm, rec_hbm, out_hbm,
                 c_in, u_buf, rec_in, left, total, resid, out_buf, c_sem, u_sem, rec_sem, out_sem,
                 *, start, count, rank):
    freqs, depth, width = u_buf.shape
    wide = 2 * rank
    span = PER_STEP * wide
    groups = depth // span
    sign = lane_sign(rank)
    factors = factor_copies(u_hbm, u_buf, u_sem)

    def arrived(f):
        return pltpu.make_async_copy(c_hbm.at[:, f], c_in.at[:, f], c_sem.at[f])

    def observed(f):
        return pltpu.make_async_copy(rec_hbm.at[f], rec_in.at[f], rec_sem.at[f])

    def result(f):
        return pltpu.make_async_copy(out_buf.at[:, f], out_hbm.at[:, f], out_sem.at[f])

    for f in range(freqs):
        arrived(f).start()
        for g in range(groups):
            factors(f, g).start()
        observed(f).start()

    def one_freq(f, carry):
        observed(f).wait()
        total[...] = -both_parts(rec_in[f].T, start, count).astype(jnp.float32)
        arrived(f).wait()

        def gather(g, inner):
            for t in range(PER_STEP):
                tile = c_in[g * PER_STEP + t, f].astype(jnp.float32)
                left[:count, t * wide:(t + 1) * wide] = (tile * sign).astype(left.dtype)
                left[count:, t * wide:(t + 1) * wide] = pltpu.roll(tile, rank, 1).astype(left.dtype)
            factors(f, g).wait()
            total[...] += jnp.dot(
                left[...], u_buf[f, pl.ds(pl.multiple_of(g * span, span), span)],
                preferred_element_type=jnp.float32,
            )
            return inner

        lax.fori_loop(0, groups, gather, 0)
        resid[...] = total[...].astype(resid.dtype)

        def spread(g, inner):
            product = lax.dot_general(
                resid[...], u_buf[f, pl.ds(pl.multiple_of(g * span, span), span)], NT,
                preferred_element_type=jnp.float32,
            )
            for t in range(PER_STEP):
                real = product[:count, t * wide:(t + 1) * wide]
                imag = product[count:, t * wide:(t + 1) * wide]
                value = sign * real + pltpu.roll(imag, rank, 1)
                out_buf[g * PER_STEP + t, f] = value.astype(out_buf.dtype)
            return inner

        lax.fori_loop(0, groups, spread, 0)
        result(f).start()
        return carry

    lax.fori_loop(0, freqs, one_freq, 0)
    for f in range(freqs):
        result(f).wait()


def grad_kernel(rank_hbm, row_hbm, cosine, sine, b_hbm, v_hbm, own_ref, *rest, count, rank):
    outs = rest[:-10]
    ranks, rows, b_in, v_buf, left, total, lags, small, b_sem, v_sem = rest[-10:]
    freqs, depth, width = v_buf.shape
    wide = 2 * rank
    span = PER_STEP * wide
    groups = depth // span
    sign = lane_sign(rank)
    index = rank_lane(rank)
    factors = factor_copies(v_hbm, v_buf, v_sem)
    rank_copy = pltpu.make_async_copy(rank_hbm, ranks, small.at[0])
    row_copy = pltpu.make_async_copy(row_hbm, rows, small.at[1])

    def returned(f):
        return pltpu.make_async_copy(b_hbm.at[:, f], b_in.at[:, f], b_sem.at[f])

    rank_copy.start()
    row_copy.start()
    for f in range(freqs):
        returned(f).start()
        for g in range(groups):
            factors(f, g).start()
    rank_copy.wait()
    row_copy.wait()

    def one_freq(f, carry):
        total[...] = jnp.zeros_like(total)
        returned(f).wait()

        def gather(g, inner):
            for t in range(PER_STEP):
                slot = g * PER_STEP + t
                tile = b_in[rows[0, slot], f].astype(jnp.float32)
                tile = jnp.where(index < ranks[f, 0, slot], tile, 0.0)
                left[:count, t * wide:(t + 1) * wide] = tile.astype(left.dtype)
                left[count:, t * wide:(t + 1) * wide] = (
                    sign * pltpu.roll(tile, rank, 1)
                ).astype(left.dtype)
            factors(f, g).wait()
            total[...] += jnp.dot(
                left[...], v_buf[f, pl.ds(pl.multiple_of(g * span, span), span)],
                preferred_element_type=jnp.float32,
            )
            return inner

        lax.fori_loop(0, groups, gather, 0)

        @pl.when(f == 0)
        def _():
            for lag in range(lags.shape[0]):
                lags[lag] = total[:count] * cosine[lag, f] - total[count:] * sine[lag, f]

        @pl.when(f > 0)
        def _():
            for lag in range(lags.shape[0]):
                share = total[:count] * cosine[lag, f] - total[count:] * sine[lag, f]
                lags[lag] += share

        return carry

    lax.fori_loop(0, freqs, one_freq, 0)
    for lag in range(lags.shape[0]):
        group, which = divmod(lag, LAG_DEV)
        ref = own_ref if group == 0 else outs[group - 1]
        ref[which] = lags[lag].astype(ref.dtype)


def finish_kernel(*refs, parts):
    out_ref = refs[-1]
    at = 0
    for p in range(len(refs[:-1]) // parts):
        group = refs[p * parts:(p + 1) * parts]
        whole = group[0][...]
        for ref in group[1:]:
            whole = whole + ref[...].astype(jnp.float32)
        count = whole.shape[1]
        out_ref[:, at:at + count] = whole
        at += count


def per_device(model_freq, recorded, v_factor, u_factor, tile_rank, tile_rows, omega):
    freqs = v_factor.shape[0]
    tiles = v_factor.shape[2]
    rank = v_factor.shape[4]
    width = v_factor.shape[5]
    columns = model_freq.shape[2]
    wide = 2 * rank
    depth = tiles * wide
    steps = tiles // PER_STEP
    groups = lax.axis_size("freq")
    freq_total = freqs * groups
    lag_total = LAG_DEV * groups
    v_flat = v_factor.reshape(freqs, depth, width)
    u_flat = u_factor.reshape(freqs, depth, width)
    order = jnp.arange(lag_total, dtype=jnp.int32) + LAG_DEV * lax.axis_index("freq")
    order = jnp.where(order >= lag_total, order - lag_total, order)
    phase = order.astype(jnp.float32)[:, None] * omega[None, :]
    cosine = jnp.cos(phase) * (2.0 / freq_total)
    sine = jnp.sin(phase) * (2.0 / freq_total)

    params = pltpu.CompilerParams(vmem_limit_bytes=VMEM_LIMIT)
    smem = pl.BlockSpec(memory_space=pltpu.SMEM)
    anywhere = pl.BlockSpec(memory_space=pl.ANY)
    vmem = pl.BlockSpec(memory_space=pltpu.VMEM)
    bf16, f32 = jnp.bfloat16, jnp.float32
    dma = pltpu.SemaphoreType.DMA
    tables = [
        pltpu.SMEM((freqs, 1, tiles), jnp.int32),
        pltpu.SMEM((1, tiles), jnp.int32),
    ]

    def cost(count, factors):
        return pl.CostEstimate(
            flops=factors * freqs * 2 * 2 * count * depth * width,
            bytes_accessed=freqs * depth * width * 2 + 4 * freqs * tiles * count * wide,
            transcendentals=0,
        )

    def blocks(count):
        return jax.ShapeDtypeStruct((tiles, freqs, count, wide), bf16)

    def coeff(start, count):
        return pl.pallas_call(
            functools.partial(coeff_kernel, start=start, count=count, rank=rank),
            in_specs=[anywhere] * 4,
            out_specs=anywhere,
            out_shape=blocks(count),
            scratch_shapes=tables + [
                pltpu.VMEM((freqs, width, columns), bf16),
                pltpu.VMEM((2 * count, width), bf16),
                pltpu.VMEM((freqs, depth, width), bf16),
                pltpu.VMEM((tiles, freqs, count, wide), bf16),
                dma((2,)), dma((freqs,)), dma((freqs, steps)), dma((freqs,)),
            ],
            compiler_params=params,
            cost_estimate=cost(count, 1),
            name="coeff",
        )(tile_rank, tile_rows, model_freq, v_flat)

    def resid(arrived, start, count):
        return pl.pallas_call(
            functools.partial(resid_kernel, start=start, count=count, rank=rank),
            in_specs=[anywhere] * 3,
            out_specs=anywhere,
            out_shape=blocks(count),
            scratch_shapes=[
                pltpu.VMEM((tiles, freqs, count, wide), bf16),
                pltpu.VMEM((freqs, depth, width), bf16),
                pltpu.VMEM((freqs, width, columns), bf16),
                pltpu.VMEM((2 * count, PER_STEP * wide), bf16),
                pltpu.VMEM((2 * count, width), f32),
                pltpu.VMEM((2 * count, width), bf16),
                pltpu.VMEM((tiles, freqs, count, wide), bf16),
                dma((freqs,)), dma((freqs, steps)), dma((freqs,)), dma((freqs,)),
            ],
            compiler_params=params,
            cost_estimate=cost(count, 2),
            name="resid",
        )(arrived, u_flat, recorded)

    def grad(returned, count):
        return pl.pallas_call(
            functools.partial(grad_kernel, count=count, rank=rank),
            in_specs=[anywhere, anywhere, smem, smem, anywhere, anywhere],
            out_specs=[vmem] * groups,
            out_shape=[jax.ShapeDtypeStruct((LAG_DEV, count, width), f32)]
            + [jax.ShapeDtypeStruct((LAG_DEV, count, width), bf16)] * (groups - 1),
            scratch_shapes=tables + [
                pltpu.VMEM((tiles, freqs, count, wide), bf16),
                pltpu.VMEM((freqs, depth, width), bf16),
                pltpu.VMEM((2 * count, PER_STEP * wide), bf16),
                pltpu.VMEM((2 * count, width), f32),
                pltpu.VMEM((lag_total, count, width), f32),
                dma((2,)), dma((freqs,)), dma((freqs, steps)),
            ],
            compiler_params=params,
            cost_estimate=cost(count, 1),
            name="grad",
        )(tile_rank, tile_rows, cosine, sine, returned, v_flat)

    def exchange(x):
        return lax.all_to_all(x, "tile", split_axis=0, concat_axis=0, tiled=True)

    def spread(shares):
        moved = [
            lax.ppermute(x, "freq", [(z, (z + d + 1) % groups) for z in range(groups)])
            for d, x in enumerate(shares[1:])
        ]
        return [shares[0]] + moved

    starts = [sum(CHUNKS[:i]) for i in range(len(CHUNKS))]
    sent = [coeff(s, n) for s, n in zip(starts, CHUNKS)]
    arrived = [exchange(x) for x in sent]
    back = [resid(x, s, n) for x, s, n in zip(arrived, starts, CHUNKS)]
    returned = [exchange(x) for x in back]
    shares = [grad(x, n) for x, n in zip(returned, CHUNKS)]
    gathered = [x for share in shares for x in spread(share)]
    total = pl.pallas_call(
        functools.partial(finish_kernel, parts=groups),
        in_specs=[vmem] * len(gathered),
        out_specs=vmem,
        out_shape=jax.ShapeDtypeStruct((LAG_DEV, SOURCES, width), f32),
        compiler_params=params,
        name="finish",
    )(*gathered)
    return jnp.swapaxes(total, 1, 2)


def solution(mesh):
    placed = (
        P("freq", "tile", None),
        P("freq", "tile", None),
        P("freq", "tile", None, None, None, None),
        P("freq", "tile", None, None, None, None),
        P("freq", "tile", None),
        P("tile", None),
        P("freq"),
    )
    return jax.shard_map(
        per_device, mesh=mesh, in_specs=placed, out_specs=P("freq", "tile", None), check_vma=False
    )
```

```python
import functools

import jax
import jax.numpy as jnp
from jax import lax
from jax.experimental import pallas as pl
from jax.experimental.pallas import tpu as pltpu
from jax.sharding import PartitionSpec as P

SOURCES = 192
LAG_DEV = 2
CHUNKS = (128, 64)
PER_STEP = 16
HEAD_VMEM = 56 * 1024 * 1024
KERNEL_VMEM = 52 * 1024 * 1024
NT = (((1,), (1,)), ((), ()))


def lane_sign(rank):
    lane = lax.broadcasted_iota(jnp.int32, (1, 2 * rank), 1)
    return jnp.where(lane < rank, 1.0, -1.0).astype(jnp.float32)


def rank_lane(rank):
    lane = lax.broadcasted_iota(jnp.int32, (1, 2 * rank), 1)
    return jnp.where(lane < rank, lane, lane - rank)


def both_parts(turned, start, count):
    half = turned.shape[0] // 2
    return jnp.concatenate(
        [turned[start:start + count], turned[half + start:half + start + count]], 0
    )


def factor_copies(hbm, buf, sems):
    freqs, depth, _ = buf.shape
    groups = sems.shape[1]
    span = depth // groups

    def copy(f, g):
        at = pl.ds(pl.multiple_of(g * span, span), span)
        return pltpu.make_async_copy(hbm.at[f, at], buf.at[f, at], sems.at[f, g])

    return copy


def coeff_kernel(rank_hbm, row_hbm, x_hbm, v_hbm, out_hbm,
                 ranks, rows, x_in, x_t, v_buf, out_buf, small, x_sem, v_sem, out_sem,
                 *, start, count, rank):
    freqs, depth, width = v_buf.shape
    wide = 2 * rank
    span = PER_STEP * wide
    groups = depth // span
    factors = factor_copies(v_hbm, v_buf, v_sem)
    rank_copy = pltpu.make_async_copy(rank_hbm, ranks, small.at[0])
    row_copy = pltpu.make_async_copy(row_hbm, rows, small.at[1])

    def model(f):
        return pltpu.make_async_copy(x_hbm.at[f], x_in.at[f], x_sem.at[f])

    def result(f):
        return pltpu.make_async_copy(out_buf.at[:, f], out_hbm.at[:, f], out_sem.at[f])

    model(0).start()
    for g in range(groups):
        factors(0, g).start()
    rank_copy.start()
    row_copy.start()
    for f in range(1, freqs):
        model(f).start()
        for g in range(groups):
            factors(f, g).start()
    sign = -lane_sign(rank)
    index = rank_lane(rank)
    rank_copy.wait()
    row_copy.wait()

    def one_freq(f, carry):
        model(f).wait()
        x_t[...] = both_parts(x_in[f].T, start, count)

        def step(g, inner):
            factors(f, g).wait()
            product = lax.dot_general(
                x_t[...], v_buf[f, pl.ds(pl.multiple_of(g * span, span), span)], NT,
                preferred_element_type=jnp.float32,
            )
            for t in range(PER_STEP):
                slot = g * PER_STEP + t
                real = product[:count, t * wide:(t + 1) * wide]
                imag = product[count:, t * wide:(t + 1) * wide]
                value = real + sign * pltpu.roll(imag, rank, 1)
                value = jnp.where(index < ranks[f, 0, slot], value, 0.0)
                out_buf[rows[0, slot], f] = value.astype(out_buf.dtype)
            return inner

        lax.fori_loop(0, groups, step, 0)
        result(f).start()
        return carry

    lax.fori_loop(0, freqs, one_freq, 0)
    for f in range(freqs):
        result(f).wait()


def resid_kernel(c_hbm, u_hbm, rec_hbm, out_hbm,
                 c_in, u_buf, rec_in, left, total, resid, out_buf, c_sem, u_sem, rec_sem, out_sem,
                 *, start, count, rank):
    freqs, depth, width = u_buf.shape
    wide = 2 * rank
    span = PER_STEP * wide
    groups = depth // span
    sign = lane_sign(rank)
    factors = factor_copies(u_hbm, u_buf, u_sem)

    def arrived(f):
        return pltpu.make_async_copy(c_hbm.at[:, f], c_in.at[:, f], c_sem.at[f])

    def observed(f):
        return pltpu.make_async_copy(rec_hbm.at[f], rec_in.at[f], rec_sem.at[f])

    def result(f):
        return pltpu.make_async_copy(out_buf.at[:, f], out_hbm.at[:, f], out_sem.at[f])

    for f in range(freqs):
        arrived(f).start()
        for g in range(groups):
            factors(f, g).start()
        observed(f).start()

    def one_freq(f, carry):
        observed(f).wait()
        total[...] = -both_parts(rec_in[f].T, start, count).astype(jnp.float32)
        arrived(f).wait()

        def gather(g, inner):
            for t in range(PER_STEP):
                tile = c_in[g * PER_STEP + t, f].astype(jnp.float32)
                left[:count, t * wide:(t + 1) * wide] = (tile * sign).astype(left.dtype)
                left[count:, t * wide:(t + 1) * wide] = pltpu.roll(tile, rank, 1).astype(left.dtype)
            factors(f, g).wait()
            total[...] += jnp.dot(
                left[...], u_buf[f, pl.ds(pl.multiple_of(g * span, span), span)],
                preferred_element_type=jnp.float32,
            )
            return inner

        lax.fori_loop(0, groups, gather, 0)
        resid[...] = total[...].astype(resid.dtype)

        def spread(g, inner):
            product = lax.dot_general(
                resid[...], u_buf[f, pl.ds(pl.multiple_of(g * span, span), span)], NT,
                preferred_element_type=jnp.float32,
            )
            for t in range(PER_STEP):
                real = product[:count, t * wide:(t + 1) * wide]
                imag = product[count:, t * wide:(t + 1) * wide]
                value = sign * real + pltpu.roll(imag, rank, 1)
                out_buf[g * PER_STEP + t, f] = value.astype(out_buf.dtype)
            return inner

        lax.fori_loop(0, groups, spread, 0)
        result(f).start()
        return carry

    lax.fori_loop(0, freqs, one_freq, 0)
    for f in range(freqs):
        result(f).wait()


def grad_kernel(rank_hbm, row_hbm, cosine, sine, b_hbm, v_hbm, own_ref, *rest, count, rank):
    outs = rest[:-10]
    ranks, rows, b_in, v_buf, left, total, lags, small, b_sem, v_sem = rest[-10:]
    freqs, depth, width = v_buf.shape
    wide = 2 * rank
    span = PER_STEP * wide
    groups = depth // span
    sign = lane_sign(rank)
    index = rank_lane(rank)
    factors = factor_copies(v_hbm, v_buf, v_sem)
    rank_copy = pltpu.make_async_copy(rank_hbm, ranks, small.at[0])
    row_copy = pltpu.make_async_copy(row_hbm, rows, small.at[1])

    def returned(f):
        return pltpu.make_async_copy(b_hbm.at[:, f], b_in.at[:, f], b_sem.at[f])

    rank_copy.start()
    row_copy.start()
    for f in range(freqs):
        returned(f).start()
        for g in range(groups):
            factors(f, g).start()
    rank_copy.wait()
    row_copy.wait()

    def one_freq(f, carry):
        total[...] = jnp.zeros_like(total)
        returned(f).wait()

        def gather(g, inner):
            for t in range(PER_STEP):
                slot = g * PER_STEP + t
                tile = b_in[rows[0, slot], f].astype(jnp.float32)
                tile = jnp.where(index < ranks[f, 0, slot], tile, 0.0)
                left[:count, t * wide:(t + 1) * wide] = tile.astype(left.dtype)
                left[count:, t * wide:(t + 1) * wide] = (
                    sign * pltpu.roll(tile, rank, 1)
                ).astype(left.dtype)
            factors(f, g).wait()
            total[...] += jnp.dot(
                left[...], v_buf[f, pl.ds(pl.multiple_of(g * span, span), span)],
                preferred_element_type=jnp.float32,
            )
            return inner

        lax.fori_loop(0, groups, gather, 0)

        @pl.when(f == 0)
        def _():
            for lag in range(lags.shape[0]):
                lags[lag] = total[:count] * cosine[lag, f] - total[count:] * sine[lag, f]

        @pl.when(f > 0)
        def _():
            for lag in range(lags.shape[0]):
                share = total[:count] * cosine[lag, f] - total[count:] * sine[lag, f]
                lags[lag] += share

        return carry

    lax.fori_loop(0, freqs, one_freq, 0)
    for lag in range(lags.shape[0]):
        group, which = divmod(lag, LAG_DEV)
        ref = own_ref if group == 0 else outs[group - 1]
        ref[which] = lags[lag].astype(ref.dtype)


def finish_kernel(*refs, parts):
    out_ref = refs[-1]
    at = 0
    for p in range(len(refs[:-1]) // parts):
        group = refs[p * parts:(p + 1) * parts]
        whole = group[0][...]
        for ref in group[1:]:
            whole = whole + ref[...].astype(jnp.float32)
        count = whole.shape[1]
        out_ref[:, at:at + count] = whole
        at += count


def per_device(model_freq, recorded, v_factor, u_factor, tile_rank, tile_rows, omega):
    freqs = v_factor.shape[0]
    tiles = v_factor.shape[2]
    rank = v_factor.shape[4]
    width = v_factor.shape[5]
    columns = model_freq.shape[2]
    wide = 2 * rank
    depth = tiles * wide
    steps = tiles // PER_STEP
    groups = lax.axis_size("freq")
    freq_total = freqs * groups
    lag_total = LAG_DEV * groups
    v_flat = v_factor.reshape(freqs, depth, width)
    u_flat = u_factor.reshape(freqs, depth, width)
    order = jnp.arange(lag_total, dtype=jnp.int32) + LAG_DEV * lax.axis_index("freq")
    order = jnp.where(order >= lag_total, order - lag_total, order)
    phase = order.astype(jnp.float32)[:, None] * omega[None, :]
    cosine = jnp.cos(phase) * (2.0 / freq_total)
    sine = jnp.sin(phase) * (2.0 / freq_total)

    head = pltpu.CompilerParams(vmem_limit_bytes=HEAD_VMEM)
    params = pltpu.CompilerParams(vmem_limit_bytes=KERNEL_VMEM)
    smem = pl.BlockSpec(memory_space=pltpu.SMEM)
    anywhere = pl.BlockSpec(memory_space=pl.ANY)
    hbm = pl.BlockSpec(memory_space=pltpu.HBM)
    vmem = pl.BlockSpec(memory_space=pltpu.VMEM)
    bf16, f32 = jnp.bfloat16, jnp.float32
    dma = pltpu.SemaphoreType.DMA
    tables = [
        pltpu.SMEM((freqs, 1, tiles), jnp.int32),
        pltpu.SMEM((1, tiles), jnp.int32),
    ]

    def cost(count, factors):
        return pl.CostEstimate(
            flops=factors * freqs * 2 * 2 * count * depth * width,
            bytes_accessed=freqs * depth * width * 2 + 4 * freqs * tiles * count * wide,
            transcendentals=0,
        )

    def blocks(count):
        return jax.ShapeDtypeStruct((tiles, freqs, count, wide), bf16)

    def coeff(start, count):
        return pl.pallas_call(
            functools.partial(coeff_kernel, start=start, count=count, rank=rank),
            in_specs=[hbm] * 4,
            out_specs=hbm,
            out_shape=blocks(count),
            scratch_shapes=tables + [
                pltpu.VMEM((freqs, width, columns), bf16),
                pltpu.VMEM((2 * count, width), bf16),
                pltpu.VMEM((freqs, depth, width), bf16),
                pltpu.VMEM((tiles, freqs, count, wide), bf16),
                dma((2,)), dma((freqs,)), dma((freqs, steps)), dma((freqs,)),
            ],
            compiler_params=head,
            cost_estimate=cost(count, 1),
            name="coeff",
        )(tile_rank, tile_rows, model_freq, v_flat)

    def resid(arrived, start, count):
        return pl.pallas_call(
            functools.partial(resid_kernel, start=start, count=count, rank=rank),
            in_specs=[anywhere, hbm, hbm],
            out_specs=hbm,
            out_shape=blocks(count),
            scratch_shapes=[
                pltpu.VMEM((tiles, freqs, count, wide), bf16),
                pltpu.VMEM((freqs, depth, width), bf16),
                pltpu.VMEM((freqs, width, columns), bf16),
                pltpu.VMEM((2 * count, PER_STEP * wide), bf16),
                pltpu.VMEM((2 * count, width), f32),
                pltpu.VMEM((2 * count, width), bf16),
                pltpu.VMEM((tiles, freqs, count, wide), bf16),
                dma((freqs,)), dma((freqs, steps)), dma((freqs,)), dma((freqs,)),
            ],
            compiler_params=params,
            cost_estimate=cost(count, 2),
            name="resid",
        )(arrived, u_flat, recorded)

    def grad(returned, count):
        return pl.pallas_call(
            functools.partial(grad_kernel, count=count, rank=rank),
            in_specs=[hbm, hbm, smem, smem, anywhere, hbm],
            out_specs=[vmem] * groups,
            out_shape=[jax.ShapeDtypeStruct((LAG_DEV, count, width), f32)]
            + [jax.ShapeDtypeStruct((LAG_DEV, count, width), bf16)] * (groups - 1),
            scratch_shapes=tables + [
                pltpu.VMEM((tiles, freqs, count, wide), bf16),
                pltpu.VMEM((freqs, depth, width), bf16),
                pltpu.VMEM((2 * count, PER_STEP * wide), bf16),
                pltpu.VMEM((2 * count, width), f32),
                pltpu.VMEM((lag_total, count, width), f32),
                dma((2,)), dma((freqs,)), dma((freqs, steps)),
            ],
            compiler_params=params,
            cost_estimate=cost(count, 1),
            name="grad",
        )(tile_rank, tile_rows, cosine, sine, returned, v_flat)

    def exchange(x):
        return lax.all_to_all(x, "tile", split_axis=0, concat_axis=0, tiled=True)

    def spread(shares):
        moved = [
            lax.ppermute(x, "freq", [(z, (z + d + 1) % groups) for z in range(groups)])
            for d, x in enumerate(shares[1:])
        ]
        return [shares[0]] + moved

    starts = [sum(CHUNKS[:i]) for i in range(len(CHUNKS))]
    sent = [coeff(s, n) for s, n in zip(starts, CHUNKS)]
    arrived = [exchange(x) for x in sent]
    back = [resid(x, s, n) for x, s, n in zip(arrived, starts, CHUNKS)]
    returned = [exchange(x) for x in back]
    shares = [grad(x, n) for x, n in zip(returned, CHUNKS)]
    gathered = [x for share in shares for x in spread(share)]
    total = pl.pallas_call(
        functools.partial(finish_kernel, parts=groups),
        in_specs=[vmem] * len(gathered),
        out_specs=vmem,
        out_shape=jax.ShapeDtypeStruct((LAG_DEV, SOURCES, width), f32),
        compiler_params=params,
        name="finish",
    )(*gathered)
    return jnp.swapaxes(total, 1, 2)


def solution(mesh):
    placed = (
        P("freq", "tile", None),
        P("freq", "tile", None),
        P("freq", "tile", None, None, None, None),
        P("freq", "tile", None, None, None, None),
        P("freq", "tile", None),
        P("tile", None),
        P("freq"),
    )
    return jax.shard_map(
        per_device, mesh=mesh, in_specs=placed, out_specs=P("freq", "tile", None), check_vma=False
    )
```

```python
import functools

import jax
import jax.numpy as jnp
from jax import lax
from jax.experimental import pallas as pl
from jax.experimental.pallas import tpu as pltpu
from jax.sharding import PartitionSpec as P

SOURCES = 192
LAG_DEV = 2
CHUNKS = (96, 96)
ROUTES = ("hop", "hop")
SIDE = 4
PER_STEP = 16
HEAD_VMEM = 56 * 1024 * 1024
KERNEL_VMEM = 48 * 1024 * 1024
SMALL_VMEM = 16 * 1024 * 1024
NT = (((1,), (1,)), ((), ()))


def lane_sign(rank):
    lane = lax.broadcasted_iota(jnp.int32, (1, 2 * rank), 1)
    return jnp.where(lane < rank, 1.0, -1.0).astype(jnp.float32)


def rank_lane(rank):
    lane = lax.broadcasted_iota(jnp.int32, (1, 2 * rank), 1)
    return jnp.where(lane < rank, lane, lane - rank)


def coordinates(tile):
    return tile // (2 * SIDE), (tile // 2) % SIDE, tile % 2


def place(route, tile):
    if route == "direct":
        return tile
    x, y, core = coordinates(lax.axis_index("tile"))
    to_x, to_y, to_core = coordinates(tile)
    step_x = lax.rem(to_x - x + SIDE, SIDE)
    step_y = lax.rem(to_y - y + SIDE, SIDE)
    first = jnp.where(core == 0, step_x, step_y)
    second = jnp.where(core == 0, step_y, step_x)
    other = jnp.where(core == to_core, 0, 1)
    return (first * SIDE + second) * 2 + other


def found(route, tile):
    if route == "direct":
        return tile
    x, y, core = coordinates(lax.axis_index("tile"))
    from_x, from_y, from_core = coordinates(tile)
    step_x = lax.rem(x - from_x + SIDE, SIDE)
    step_y = lax.rem(y - from_y + SIDE, SIDE)
    first = jnp.where(from_core == 0, step_x, step_y)
    second = jnp.where(from_core == 0, step_y, step_x)
    return jnp.where(core == from_core, 0, SIDE * SIDE) + second * SIDE + first


def leaving(route, refs, buf, sems, f):
    span = buf.shape[0] // len(refs)
    return [
        pltpu.make_async_copy(buf.at[pl.ds(n * span, span), f], ref.at[:, f], sems.at[f, n])
        for n, ref in enumerate(refs)
    ]


def arriving(route, refs, buf, sems, f):
    if route == "direct":
        return [pltpu.make_async_copy(refs[0].at[:, f], buf.at[:, f], sems.at[f, 0])]
    own = [
        pltpu.make_async_copy(
            ref.at[:, 0, f], buf.at[pl.ds(n * SIDE, SIDE), f], sems.at[f, n]
        )
        for n, ref in enumerate(refs[:-1])
    ]
    last = pltpu.make_async_copy(
        refs[-1].at[:, f], buf.at[pl.ds(SIDE * SIDE, SIDE * SIDE), f], sems.at[f, SIDE]
    )
    return own + [last]


def both_parts(turned, start, count):
    half = turned.shape[0] // 2
    return jnp.concatenate(
        [turned[start:start + count], turned[half + start:half + start + count]], 0
    )


def factor_copies(hbm, buf, sems):
    freqs, depth, _ = buf.shape
    groups = sems.shape[1]
    span = depth // groups

    def copy(f, g):
        at = pl.ds(pl.multiple_of(g * span, span), span)
        return pltpu.make_async_copy(hbm.at[f, at], buf.at[f, at], sems.at[f, g])

    return copy


def coeff_kernel(rank_hbm, row_hbm, x_hbm, v_hbm, *rest, start, count, rank, route):
    outs = rest[:-10]
    ranks, rows, x_in, x_t, v_buf, out_buf, small, x_sem, v_sem, out_sem = rest[-10:]
    freqs, depth, width = v_buf.shape
    wide = 2 * rank
    span = PER_STEP * wide
    groups = depth // span
    factors = factor_copies(v_hbm, v_buf, v_sem)
    rank_copy = pltpu.make_async_copy(rank_hbm, ranks, small.at[0])
    row_copy = pltpu.make_async_copy(row_hbm, rows, small.at[1])

    def model(f):
        return pltpu.make_async_copy(x_hbm.at[f], x_in.at[f], x_sem.at[f])

    def results(f):
        return leaving(route, outs, out_buf, out_sem, f)

    model(0).start()
    for g in range(groups):
        factors(0, g).start()
    rank_copy.start()
    row_copy.start()
    for f in range(1, freqs):
        model(f).start()
        for g in range(groups):
            factors(f, g).start()
    sign = -lane_sign(rank)
    index = rank_lane(rank)
    rank_copy.wait()
    row_copy.wait()

    def one_freq(f, carry):
        model(f).wait()
        x_t[...] = both_parts(x_in[f].T, start, count)

        def step(g, inner):
            factors(f, g).wait()
            product = lax.dot_general(
                x_t[...], v_buf[f, pl.ds(pl.multiple_of(g * span, span), span)], NT,
                preferred_element_type=jnp.float32,
            )
            for t in range(PER_STEP):
                slot = g * PER_STEP + t
                real = product[:count, t * wide:(t + 1) * wide]
                imag = product[count:, t * wide:(t + 1) * wide]
                value = real + sign * pltpu.roll(imag, rank, 1)
                value = jnp.where(index < ranks[f, 0, slot], value, 0.0)
                out_buf[place(route, rows[0, slot]), f] = value.astype(out_buf.dtype)
            return inner

        lax.fori_loop(0, groups, step, 0)
        for copy in results(f):
            copy.start()
        return carry

    lax.fori_loop(0, freqs, one_freq, 0)
    for f in range(freqs):
        for copy in results(f):
            copy.wait()


def resid_kernel(*refs, start, count, rank, route, parts):
    (c_in, u_buf, rec_in, left, total, resid, out_buf,
     c_sem, u_sem, rec_sem, out_sem) = refs[-11:]
    coming = refs[:parts]
    u_hbm, rec_hbm = refs[parts:parts + 2]
    outs = refs[parts + 2:-11]
    freqs, depth, width = u_buf.shape
    wide = 2 * rank
    span = PER_STEP * wide
    groups = depth // span
    sign = lane_sign(rank)
    factors = factor_copies(u_hbm, u_buf, u_sem)

    def arrived(f):
        return arriving(route, coming, c_in, c_sem, f)

    def observed(f):
        return pltpu.make_async_copy(rec_hbm.at[f], rec_in.at[f], rec_sem.at[f])

    def results(f):
        return leaving(route, outs, out_buf, out_sem, f)

    for f in range(freqs):
        for copy in arrived(f):
            copy.start()
        for g in range(groups):
            factors(f, g).start()
        observed(f).start()

    def one_freq(f, carry):
        observed(f).wait()
        total[...] = -both_parts(rec_in[f].T, start, count).astype(jnp.float32)
        for copy in arrived(f):
            copy.wait()

        def gather(g, inner):
            for t in range(PER_STEP):
                tile = c_in[found(route, g * PER_STEP + t), f].astype(jnp.float32)
                left[:count, t * wide:(t + 1) * wide] = (tile * sign).astype(left.dtype)
                left[count:, t * wide:(t + 1) * wide] = pltpu.roll(tile, rank, 1).astype(left.dtype)
            factors(f, g).wait()
            total[...] += jnp.dot(
                left[...], u_buf[f, pl.ds(pl.multiple_of(g * span, span), span)],
                preferred_element_type=jnp.float32,
            )
            return inner

        lax.fori_loop(0, groups, gather, 0)
        resid[...] = total[...].astype(resid.dtype)

        def spread(g, inner):
            product = lax.dot_general(
                resid[...], u_buf[f, pl.ds(pl.multiple_of(g * span, span), span)], NT,
                preferred_element_type=jnp.float32,
            )
            for t in range(PER_STEP):
                real = product[:count, t * wide:(t + 1) * wide]
                imag = product[count:, t * wide:(t + 1) * wide]
                value = sign * real + pltpu.roll(imag, rank, 1)
                out_buf[place(route, g * PER_STEP + t), f] = value.astype(out_buf.dtype)
            return inner

        lax.fori_loop(0, groups, spread, 0)
        for copy in results(f):
            copy.start()
        return carry

    lax.fori_loop(0, freqs, one_freq, 0)
    for f in range(freqs):
        for copy in results(f):
            copy.wait()


def grad_kernel(rank_hbm, row_hbm, cosine, sine, v_hbm, *rest, count, rank, route, parts):
    coming = rest[:parts]
    own_ref = rest[parts]
    outs = rest[parts + 1:-10]
    ranks, rows, b_in, v_buf, left, total, lags, small, b_sem, v_sem = rest[-10:]
    freqs, depth, width = v_buf.shape
    wide = 2 * rank
    span = PER_STEP * wide
    groups = depth // span
    sign = lane_sign(rank)
    index = rank_lane(rank)
    factors = factor_copies(v_hbm, v_buf, v_sem)
    rank_copy = pltpu.make_async_copy(rank_hbm, ranks, small.at[0])
    row_copy = pltpu.make_async_copy(row_hbm, rows, small.at[1])

    def returned(f):
        return arriving(route, coming, b_in, b_sem, f)

    rank_copy.start()
    row_copy.start()
    for f in range(freqs):
        for copy in returned(f):
            copy.start()
        for g in range(groups):
            factors(f, g).start()
    rank_copy.wait()
    row_copy.wait()

    def one_freq(f, carry):
        total[...] = jnp.zeros_like(total)
        for copy in returned(f):
            copy.wait()

        def gather(g, inner):
            for t in range(PER_STEP):
                slot = g * PER_STEP + t
                tile = b_in[found(route, rows[0, slot]), f].astype(jnp.float32)
                tile = jnp.where(index < ranks[f, 0, slot], tile, 0.0)
                left[:count, t * wide:(t + 1) * wide] = tile.astype(left.dtype)
                left[count:, t * wide:(t + 1) * wide] = (
                    sign * pltpu.roll(tile, rank, 1)
                ).astype(left.dtype)
            factors(f, g).wait()
            total[...] += jnp.dot(
                left[...], v_buf[f, pl.ds(pl.multiple_of(g * span, span), span)],
                preferred_element_type=jnp.float32,
            )
            return inner

        lax.fori_loop(0, groups, gather, 0)

        @pl.when(f == 0)
        def _():
            for lag in range(lags.shape[0]):
                lags[lag] = total[:count] * cosine[lag, f] - total[count:] * sine[lag, f]

        @pl.when(f > 0)
        def _():
            for lag in range(lags.shape[0]):
                share = total[:count] * cosine[lag, f] - total[count:] * sine[lag, f]
                lags[lag] += share

        return carry

    lax.fori_loop(0, freqs, one_freq, 0)
    for lag in range(lags.shape[0]):
        group, which = divmod(lag, LAG_DEV)
        ref = own_ref if group == 0 else outs[group - 1]
        ref[which] = lags[lag].astype(ref.dtype)


def turn_kernel(*refs):
    for e, out in enumerate(refs[SIDE:]):
        for d, ref in enumerate(refs[:SIDE]):
            out[d] = ref[e]


def swap_kernel(*refs):
    for e, ref in enumerate(refs[:SIDE]):
        refs[SIDE][e * SIDE:(e + 1) * SIDE] = ref[:, 1]


def finish_kernel(*refs, parts):
    out_ref = refs[-1]
    at = 0
    for p in range(len(refs[:-1]) // parts):
        group = refs[p * parts:(p + 1) * parts]
        whole = group[0][...]
        for ref in group[1:]:
            whole = whole + ref[...].astype(jnp.float32)
        count = whole.shape[1]
        out_ref[:, at:at + count] = whole
        at += count


def per_device(model_freq, recorded, v_factor, u_factor, tile_rank, tile_rows, omega):
    freqs = v_factor.shape[0]
    tiles = v_factor.shape[2]
    rank = v_factor.shape[4]
    width = v_factor.shape[5]
    columns = model_freq.shape[2]
    wide = 2 * rank
    depth = tiles * wide
    steps = tiles // PER_STEP
    groups = lax.axis_size("freq")
    freq_total = freqs * groups
    lag_total = LAG_DEV * groups
    v_flat = v_factor.reshape(freqs, depth, width)
    u_flat = u_factor.reshape(freqs, depth, width)
    order = jnp.arange(lag_total, dtype=jnp.int32) + LAG_DEV * lax.axis_index("freq")
    order = jnp.where(order >= lag_total, order - lag_total, order)
    phase = order.astype(jnp.float32)[:, None] * omega[None, :]
    cosine = jnp.cos(phase) * (2.0 / freq_total)
    sine = jnp.sin(phase) * (2.0 / freq_total)

    head = pltpu.CompilerParams(vmem_limit_bytes=HEAD_VMEM)
    params = pltpu.CompilerParams(vmem_limit_bytes=KERNEL_VMEM)
    small = pltpu.CompilerParams(vmem_limit_bytes=SMALL_VMEM)
    smem = pl.BlockSpec(memory_space=pltpu.SMEM)
    anywhere = pl.BlockSpec(memory_space=pl.ANY)
    hbm = pl.BlockSpec(memory_space=pltpu.HBM)
    vmem = pl.BlockSpec(memory_space=pltpu.VMEM)
    bf16, f32 = jnp.bfloat16, jnp.float32
    dma = pltpu.SemaphoreType.DMA
    tables = [
        pltpu.SMEM((freqs, 1, tiles), jnp.int32),
        pltpu.SMEM((1, tiles), jnp.int32),
    ]

    def cost(count, factors):
        return pl.CostEstimate(
            flops=factors * freqs * 2 * 2 * count * depth * width,
            bytes_accessed=freqs * depth * width * 2 + 4 * freqs * tiles * count * wide,
            transcendentals=0,
        )

    def blocks(count, route):
        sent = SIDE if route == "hop" else 1
        return [jax.ShapeDtypeStruct((tiles // sent, freqs, count, wide), bf16)] * sent

    def coeff(start, count, route):
        return pl.pallas_call(
            functools.partial(coeff_kernel, start=start, count=count, rank=rank, route=route),
            in_specs=[hbm] * 4,
            out_specs=[hbm] * len(blocks(count, route)),
            out_shape=blocks(count, route),
            scratch_shapes=tables + [
                pltpu.VMEM((freqs, width, columns), bf16),
                pltpu.VMEM((2 * count, width), bf16),
                pltpu.VMEM((freqs, depth, width), bf16),
                pltpu.VMEM((tiles, freqs, count, wide), bf16),
                dma((2,)), dma((freqs,)), dma((freqs, steps)), dma((freqs, SIDE)),
            ],
            compiler_params=head,
            cost_estimate=cost(count, 1),
            name="coeff",
        )(tile_rank, tile_rows, model_freq, v_flat)

    def resid(arrived, start, count, route):
        return pl.pallas_call(
            functools.partial(
                resid_kernel, start=start, count=count, rank=rank, route=route,
                parts=len(arrived),
            ),
            in_specs=[anywhere] * len(arrived) + [hbm, hbm],
            out_specs=[hbm] * len(blocks(count, route)),
            out_shape=blocks(count, route),
            scratch_shapes=[
                pltpu.VMEM((tiles, freqs, count, wide), bf16),
                pltpu.VMEM((freqs, depth, width), bf16),
                pltpu.VMEM((freqs, width, columns), bf16),
                pltpu.VMEM((2 * count, PER_STEP * wide), bf16),
                pltpu.VMEM((2 * count, width), f32),
                pltpu.VMEM((2 * count, width), bf16),
                pltpu.VMEM((tiles, freqs, count, wide), bf16),
                dma((freqs, SIDE + 1)), dma((freqs, steps)), dma((freqs,)), dma((freqs, SIDE)),
            ],
            compiler_params=params,
            cost_estimate=cost(count, 2),
            name="resid",
        )(*arrived, u_flat, recorded)

    def grad(returned, count, route):
        return pl.pallas_call(
            functools.partial(
                grad_kernel, count=count, rank=rank, route=route, parts=len(returned)
            ),
            in_specs=[hbm, hbm, smem, smem, hbm] + [anywhere] * len(returned),
            out_specs=[vmem] * groups,
            out_shape=[jax.ShapeDtypeStruct((LAG_DEV, count, width), f32)]
            + [jax.ShapeDtypeStruct((LAG_DEV, count, width), bf16)] * (groups - 1),
            scratch_shapes=tables + [
                pltpu.VMEM((tiles, freqs, count, wide), bf16),
                pltpu.VMEM((freqs, depth, width), bf16),
                pltpu.VMEM((2 * count, PER_STEP * wide), bf16),
                pltpu.VMEM((2 * count, width), f32),
                pltpu.VMEM((lag_total, count, width), f32),
                dma((2,)), dma((freqs, SIDE + 1)), dma((freqs, steps)),
            ],
            compiler_params=params,
            cost_estimate=cost(count, 1),
            name="grad",
        )(tile_rank, tile_rows, cosine, sine, v_flat, *returned)

    def number(x, y, core):
        return ((x % SIDE) * SIDE + y % SIDE) * 2 + core

    def along(step, first):
        return [
            (
                number(x, y, core),
                number(x + step, y, core) if (core == 0) == first else number(x, y + step, core),
            )
            for x in range(SIDE)
            for y in range(SIDE)
            for core in range(2)
        ]

    def exchange(parts, route):
        if route == "direct":
            return [lax.all_to_all(parts[0], "tile", split_axis=0, concat_axis=0, tiled=True)]
        shape = (SIDE, 2) + parts[0].shape[1:]
        here = [parts[0]] + [
            lax.ppermute(parts[d], "tile", along(d, True)) for d in range(1, SIDE)
        ]
        here = [x.reshape(shape) for x in here]
        onward = pl.pallas_call(
            turn_kernel,
            in_specs=[vmem] * SIDE,
            out_specs=[vmem] * SIDE,
            out_shape=[jax.ShapeDtypeStruct(shape, bf16)] * SIDE,
            compiler_params=small,
            name="turn",
        )(*here)
        there = [onward[0]] + [
            lax.ppermute(onward[e], "tile", along(e, False)) for e in range(1, SIDE)
        ]
        crossing = pl.pallas_call(
            swap_kernel,
            in_specs=[vmem] * SIDE,
            out_specs=vmem,
            out_shape=jax.ShapeDtypeStruct((SIDE * SIDE,) + shape[2:], bf16),
            compiler_params=small,
            name="swap",
        )(*there)
        swapped = lax.ppermute(crossing, "tile", [(n, n ^ 1) for n in range(tiles)])
        return there + [swapped]

    def spread(shares):
        moved = [
            lax.ppermute(x, "freq", [(z, (z + d + 1) % groups) for z in range(groups)])
            for d, x in enumerate(shares[1:])
        ]
        return [shares[0]] + moved

    starts = [sum(CHUNKS[:i]) for i in range(len(CHUNKS))]
    chunks = list(zip(starts, CHUNKS, ROUTES))
    sent = [coeff(s, n, r) for s, n, r in chunks]
    arrived = [exchange(x, r) for x, r in zip(sent, ROUTES)]
    back = [resid(x, *chunk) for x, chunk in zip(arrived, chunks)]
    returned = [exchange(x, r) for x, r in zip(back, ROUTES)]
    shares = [grad(x, n, r) for x, (_, n, r) in zip(returned, chunks)]
    gathered = [x for share in shares for x in spread(share)]
    total = pl.pallas_call(
        functools.partial(finish_kernel, parts=groups),
        in_specs=[vmem] * len(gathered),
        out_specs=vmem,
        out_shape=jax.ShapeDtypeStruct((LAG_DEV, SOURCES, width), f32),
        compiler_params=params,
        name="finish",
    )(*gathered)
    return jnp.swapaxes(total, 1, 2)


def solution(mesh):
    placed = (
        P("freq", "tile", None),
        P("freq", "tile", None),
        P("freq", "tile", None, None, None, None),
        P("freq", "tile", None, None, None, None),
        P("freq", "tile", None),
        P("tile", None),
        P("freq"),
    )
    return jax.shard_map(
        per_device, mesh=mesh, in_specs=placed, out_specs=P("freq", "tile", None), check_vma=False
    )
```

```python
import functools

import jax
import jax.numpy as jnp
from jax import lax
from jax.experimental import pallas as pl
from jax.experimental.pallas import tpu as pltpu
from jax.sharding import PartitionSpec as P


SOURCES = 192
LAG_DEV = 2
CHUNKS = (112, 80)
ROUTES = ("direct", "hop")
SIDE = 4
PER_STEP = 8
ROWS = 16
HEAD_VMEM = 40 * 1024 * 1024
KERNEL_VMEM = 40 * 1024 * 1024
SMALL_VMEM = 16 * 1024 * 1024
NT = (((1,), (1,)), ((), ()))


def lane_sign(rank):
    lane = lax.broadcasted_iota(jnp.int32, (1, 2 * rank), 1)
    return jnp.where(lane < rank, 1.0, -1.0).astype(jnp.float32)


def rank_lane(rank):
    lane = lax.broadcasted_iota(jnp.int32, (1, 2 * rank), 1)
    return jnp.where(lane < rank, lane, lane - rank)


def coordinates(tile):
    return tile // (2 * SIDE), (tile // 2) % SIDE, tile % 2


def place(route, tile):
    if route == "direct":
        return tile
    x, y, core = coordinates(lax.axis_index("tile"))
    to_x, to_y, to_core = coordinates(tile)
    step_x = lax.rem(to_x - x + SIDE, SIDE)
    step_y = lax.rem(to_y - y + SIDE, SIDE)
    first = jnp.where(core == 0, step_x, step_y)
    second = jnp.where(core == 0, step_y, step_x)
    other = jnp.where(core == to_core, 0, 1)
    return (first * SIDE + second) * 2 + other


def found(route, tile):
    if route == "direct":
        return tile
    x, y, core = coordinates(lax.axis_index("tile"))
    from_x, from_y, from_core = coordinates(tile)
    step_x = lax.rem(x - from_x + SIDE, SIDE)
    step_y = lax.rem(y - from_y + SIDE, SIDE)
    first = jnp.where(from_core == 0, step_x, step_y)
    second = jnp.where(from_core == 0, step_y, step_x)
    return jnp.where(core == from_core, 0, SIDE * SIDE) + second * SIDE + first


def leaving(refs, buf, sems, f):
    span = buf.shape[0] // len(refs)
    return [
        pltpu.make_async_copy(buf.at[pl.ds(n * span, span), f], ref.at[:, f], sems.at[f, n])
        for n, ref in enumerate(refs)
    ]


def arriving(route, refs, buf, sems, f):
    if route == "direct":
        return [pltpu.make_async_copy(refs[0].at[:, f], buf.at[:, f], sems.at[f, 0])]
    own = [
        pltpu.make_async_copy(
            ref.at[:, 0, f], buf.at[pl.ds(n * SIDE, SIDE), f], sems.at[f, n]
        )
        for n, ref in enumerate(refs[:-1])
    ]
    last = pltpu.make_async_copy(
        refs[-1].at[:, f], buf.at[pl.ds(SIDE * SIDE, SIDE * SIDE), f], sems.at[f, SIDE]
    )
    return own + [last]


def halves_swapped(tile, rank):
    return jnp.concatenate([tile[:, rank:], tile[:, :rank]], 1)


def both_parts(turned, start, count):
    half = turned.shape[0] // 2
    return jnp.concatenate(
        [turned[start:start + count], turned[half + start:half + start + count]], 0
    )


def factor_copies(hbm, buf, sems):
    _, depth, _ = buf.shape
    groups = sems.shape[1]
    span = depth // groups

    def copy(f, g):
        at = pl.ds(pl.multiple_of(g * span, span), span)
        return pltpu.make_async_copy(hbm.at[f, at], buf.at[f, at], sems.at[f, g])

    return copy


def coeff_kernel(rank_hbm, row_hbm, x_hbm, v_hbm, *rest, start, count, rank, route):
    outs = rest[:-10]
    ranks, rows, x_in, x_t, v_buf, out_buf, small, x_sem, v_sem, out_sem = rest[-10:]
    freqs, depth, _ = v_buf.shape
    wide = 2 * rank
    span = PER_STEP * wide
    groups = depth // span
    factors = factor_copies(v_hbm, v_buf, v_sem)
    rank_copy = pltpu.make_async_copy(rank_hbm, ranks, small.at[0])
    row_copy = pltpu.make_async_copy(row_hbm, rows, small.at[1])

    def model(f):
        return pltpu.make_async_copy(x_hbm.at[f], x_in.at[f], x_sem.at[f])

    def results(f):
        return leaving(outs, out_buf, out_sem, f)

    model(0).start()
    for g in range(groups):
        factors(0, g).start()
    rank_copy.start()
    row_copy.start()
    for f in range(1, freqs):
        model(f).start()
        for g in range(groups):
            factors(f, g).start()
    sign = -lane_sign(rank)
    index = rank_lane(rank)
    rank_copy.wait()
    row_copy.wait()

    def one_freq(f, carry):
        model(f).wait()
        x_t[...] = both_parts(x_in[f].T, start, count)

        for g in range(groups):
            factors(f, g).wait()
        for g in range(groups):
            product = lax.dot_general(
                x_t[...], v_buf[f, g * span:(g + 1) * span], NT,
                preferred_element_type=jnp.float32,
            )
            for t in range(PER_STEP):
                slot = g * PER_STEP + t
                real = product[:count, t * wide:(t + 1) * wide]
                imag = product[count:, t * wide:(t + 1) * wide]
                value = real + sign * pltpu.roll(imag, rank, 1)
                value = jnp.where(index < ranks[f, 0, slot], value, 0.0)
                out_buf[place(route, rows[0, slot]), f] = value.astype(out_buf.dtype)
        for copy in results(f):
            copy.start()
        return carry

    lax.fori_loop(0, freqs, one_freq, 0)
    for f in range(freqs):
        for copy in results(f):
            copy.wait()


def resid_kernel(*refs, start, count, rank, route, parts):
    (c_in, u_buf, rec_in, left, resid, out_buf,
     c_sem, u_sem, rec_sem, out_sem) = refs[-10:]
    coming = refs[:parts]
    u_hbm, rec_hbm = refs[parts:parts + 2]
    outs = refs[parts + 2:-10]
    freqs, depth, _ = u_buf.shape
    wide = 2 * rank
    span = PER_STEP * wide
    groups = depth // span
    sign = lane_sign(rank)
    factors = factor_copies(u_hbm, u_buf, u_sem)

    def arrived(f):
        return arriving(route, coming, c_in, c_sem, f)

    def observed(f):
        return pltpu.make_async_copy(rec_hbm.at[f], rec_in.at[f], rec_sem.at[f])

    def results(f):
        return leaving(outs, out_buf, out_sem, f)

    for f in range(freqs):
        for copy in arrived(f):
            copy.start()
        for g in range(groups):
            factors(f, g).start()
        observed(f).start()

    def gather(f):
        for slot in range(depth // wide):
            at = slice(slot * wide, (slot + 1) * wide)
            tile = c_in[found(route, slot), f]
            left[f, :count, at] = tile * sign.astype(tile.dtype)
            left[f, count:, at] = halves_swapped(tile, rank)

    def forward(f):
        total = -both_parts(rec_in[f].T, start, count).astype(jnp.float32)
        for g in range(groups):
            part = slice(g * span, (g + 1) * span)
            total = total + jnp.dot(
                left[f, :, part], u_buf[f, part], preferred_element_type=jnp.float32
            )
        resid[f] = total.astype(resid.dtype)

    def spread(f):
        for g in range(groups):
            product = lax.dot_general(
                resid[f], u_buf[f, g * span:(g + 1) * span], NT,
                preferred_element_type=jnp.float32,
            )
            for t in range(PER_STEP):
                real = product[:count, t * wide:(t + 1) * wide]
                imag = product[count:, t * wide:(t + 1) * wide]
                value = sign * real + pltpu.roll(imag, rank, 1)
                out_buf[place(route, g * PER_STEP + t), f] = value.astype(out_buf.dtype)

    def ready(f):
        for g in range(groups):
            factors(f, g).wait()

    for f in range(freqs):
        observed(f).wait()
        for copy in arrived(f):
            copy.wait()
    gather(0)
    ready(0)
    forward(0)
    for f in range(freqs):
        if f + 1 < freqs:
            gather(f + 1)
            ready(f + 1)
            forward(f + 1)
        spread(f)
        for copy in results(f):
            copy.start()
    for f in range(freqs):
        for copy in results(f):
            copy.wait()


def grad_kernel(rank_hbm, row_hbm, omega, v_hbm, *rest, count, rank, route, parts):
    coming = rest[:parts]
    own_ref = rest[parts]
    outs = rest[parts + 1:-10]
    ranks, rows, b_in, v_buf, left, total, waves, small, b_sem, v_sem = rest[-10:]
    freqs, depth, width = v_buf.shape
    wide = 2 * rank
    span = PER_STEP * wide
    groups = depth // span
    sign = lane_sign(rank)
    index = rank_lane(rank)
    factors = factor_copies(v_hbm, v_buf, v_sem)
    rank_copy = pltpu.make_async_copy(rank_hbm, ranks, small.at[0])
    row_copy = pltpu.make_async_copy(row_hbm, rows, small.at[1])

    def returned(f):
        return arriving(route, coming, b_in, b_sem, f)

    rank_copy.start()
    row_copy.start()
    for f in range(freqs):
        for copy in returned(f):
            copy.start()
        for g in range(groups):
            factors(f, g).start()
    rank_copy.wait()
    row_copy.wait()

    def gather(f):
        for slot in range(depth // wide):
            at = slice(slot * wide, (slot + 1) * wide)
            tile = b_in[found(route, rows[0, slot]), f]
            keep = jnp.where(index < ranks[f, 0, slot], 1.0, 0.0)
            left[f, :count, at] = tile * keep.astype(tile.dtype)
            turned = halves_swapped(tile, rank)
            left[f, count:, at] = turned * (sign * keep).astype(tile.dtype)

    def product(f):
        for g in range(groups):
            part = slice(g * span, (g + 1) * span)
            term = jnp.dot(left[f, :, part], v_buf[f, part], preferred_element_type=jnp.float32)
            total[f] = term if g == 0 else total[f] + term

    def ready(f):
        for g in range(groups):
            factors(f, g).wait()

    for f in range(freqs):
        for copy in returned(f):
            copy.wait()
    gather(0)
    for f in range(freqs):
        ready(f)
        product(f)
        if f + 1 < freqs:
            gather(f + 1)

    lag_total = LAG_DEV * (len(outs) + 1)
    order = lax.broadcasted_iota(jnp.int32, (lag_total, width), 0) + LAG_DEV * lax.axis_index("freq")
    order = jnp.where(order >= lag_total, order - lag_total, order).astype(jnp.float32)
    scale = 2.0 / (freqs * lag_total // LAG_DEV)
    for f in range(freqs):
        waves[0, f] = jnp.cos(order * omega[f]) * scale
        waves[1, f] = jnp.sin(order * omega[f]) * scale

    def combine(n, carry):
        at = pl.ds(pl.multiple_of(n * ROWS, ROWS), ROWS)
        reals = [total[f, at] for f in range(freqs)]
        imags = [total[f, pl.ds(pl.multiple_of(count + n * ROWS, ROWS), ROWS)] for f in range(freqs)]
        for lag in range(lag_total):
            group, which = divmod(lag, LAG_DEV)
            ref = own_ref if group == 0 else outs[group - 1]
            share = None
            for f in range(freqs):
                term = reals[f] * waves[0, f, lag:lag + 1] - imags[f] * waves[1, f, lag:lag + 1]
                share = term if share is None else share + term
            ref[which, at] = share.astype(ref.dtype)
        return carry

    lax.fori_loop(0, count // ROWS, combine, 0)


def turn_kernel(*refs):
    for e, out in enumerate(refs[-SIDE:]):
        for d, ref in enumerate(refs[:SIDE]):
            out[d] = ref[e]


def swap_kernel(*refs):
    for e, ref in enumerate(refs[:SIDE]):
        refs[-1][e * SIDE:(e + 1) * SIDE] = ref[:, 1]


def finish_kernel(*refs, parts):
    out_ref = refs[-1]
    at = 0
    for p in range(len(refs[:-1]) // parts):
        group = refs[p * parts:(p + 1) * parts]
        whole = group[0][...]
        for ref in group[1:]:
            whole = whole + ref[...].astype(jnp.float32)
        count = whole.shape[1]
        out_ref[:, at:at + count] = whole
        at += count


def per_device(model_freq, recorded, v_factor, u_factor, tile_rank, tile_rows, omega):
    freqs = v_factor.shape[0]
    tiles = v_factor.shape[2]
    rank = v_factor.shape[4]
    width = v_factor.shape[5]
    columns = model_freq.shape[2]
    wide = 2 * rank
    depth = tiles * wide
    steps = tiles // PER_STEP
    groups = lax.axis_size("freq")
    lag_total = LAG_DEV * groups
    v_flat = v_factor.reshape(freqs, depth, width)
    u_flat = u_factor.reshape(freqs, depth, width)
    head = pltpu.CompilerParams(vmem_limit_bytes=HEAD_VMEM)
    params = pltpu.CompilerParams(vmem_limit_bytes=KERNEL_VMEM)
    small = pltpu.CompilerParams(vmem_limit_bytes=SMALL_VMEM)
    smem = pl.BlockSpec(memory_space=pltpu.SMEM)
    anywhere = pl.BlockSpec(memory_space=pl.ANY)
    hbm = pl.BlockSpec(memory_space=pltpu.HBM)
    vmem = pl.BlockSpec(memory_space=pltpu.VMEM)
    bf16, f32 = jnp.bfloat16, jnp.float32
    dma = pltpu.SemaphoreType.DMA
    tables = [
        pltpu.SMEM((freqs, 1, tiles), jnp.int32),
        pltpu.SMEM((1, tiles), jnp.int32),
    ]

    def in_hbm(x):
        return pltpu.with_memory_space_constraint(x, pltpu.HBM)

    def cost(count, factors):
        return pl.CostEstimate(
            flops=factors * freqs * 2 * 2 * count * depth * width,
            bytes_accessed=freqs * depth * width * 2 + 4 * freqs * tiles * count * wide,
            transcendentals=0,
        )

    def blocks(count, route):
        if route == "direct":
            return [pltpu.HBM((tiles, freqs, count, wide), bf16)]
        return [jax.ShapeDtypeStruct((tiles // SIDE, freqs, count, wide), bf16)] * SIDE

    def coeff(start, count, route):
        return pl.pallas_call(
            functools.partial(coeff_kernel, start=start, count=count, rank=rank, route=route),
            in_specs=[hbm] * 4,
            out_specs=[hbm] * len(blocks(count, route)),
            out_shape=blocks(count, route),
            scratch_shapes=tables + [
                pltpu.VMEM((freqs, width, columns), bf16),
                pltpu.VMEM((2 * count, width), bf16),
                pltpu.VMEM((freqs, depth, width), bf16),
                pltpu.VMEM((tiles, freqs, count, wide), bf16),
                dma((2,)), dma((freqs,)), dma((freqs, steps)), dma((freqs, SIDE)),
            ],
            compiler_params=head,
            cost_estimate=cost(count, 1),
            name="coeff",
        )(in_hbm(tile_rank), in_hbm(tile_rows), in_hbm(model_freq), in_hbm(v_flat))

    def resid(arrived, start, count, route):
        return pl.pallas_call(
            functools.partial(
                resid_kernel, start=start, count=count, rank=rank, route=route,
                parts=len(arrived),
            ),
            in_specs=[anywhere] * len(arrived) + [hbm, hbm],
            out_specs=[hbm] * len(blocks(count, route)),
            out_shape=blocks(count, route),
            scratch_shapes=[
                pltpu.VMEM((tiles, freqs, count, wide), bf16),
                pltpu.VMEM((freqs, depth, width), bf16),
                pltpu.VMEM((freqs, width, columns), bf16),
                pltpu.VMEM((freqs, 2 * count, depth), bf16),
                pltpu.VMEM((freqs, 2 * count, width), bf16),
                pltpu.VMEM((tiles, freqs, count, wide), bf16),
                dma((freqs, SIDE + 1)), dma((freqs, steps)), dma((freqs,)), dma((freqs, SIDE)),
            ],
            compiler_params=params,
            cost_estimate=cost(count, 2),
            name="resid",
        )(*arrived, in_hbm(u_flat), in_hbm(recorded))

    def grad(returned, count, route):
        return pl.pallas_call(
            functools.partial(
                grad_kernel, count=count, rank=rank, route=route, parts=len(returned)
            ),
            in_specs=[hbm, hbm, smem, hbm] + [anywhere] * len(returned),
            out_specs=[vmem] * groups,
            out_shape=[jax.ShapeDtypeStruct((LAG_DEV, count, width), f32)]
            + [jax.ShapeDtypeStruct((LAG_DEV, count, width), bf16)] * (groups - 1),
            scratch_shapes=tables + [
                pltpu.VMEM((tiles, freqs, count, wide), bf16),
                pltpu.VMEM((freqs, depth, width), bf16),
                pltpu.VMEM((freqs, 2 * count, depth), bf16),
                pltpu.VMEM((freqs, 2 * count, width), f32),
                pltpu.VMEM((2, freqs, lag_total, width), f32),
                dma((2,)), dma((freqs, SIDE + 1)), dma((freqs, steps)),
            ],
            compiler_params=params,
            cost_estimate=cost(count, 1),
            name="grad",
        )(in_hbm(tile_rank), in_hbm(tile_rows), omega, in_hbm(v_flat), *returned)

    def number(x, y, core):
        return ((x % SIDE) * SIDE + y % SIDE) * 2 + core

    def along(step, first):
        return [
            (
                number(x, y, core),
                number(x + step, y, core) if (core == 0) == first else number(x, y + step, core),
            )
            for x in range(SIDE)
            for y in range(SIDE)
            for core in range(2)
        ]

    def hop(parts, first):
        return [parts[0]] + [
            lax.ppermute(parts[d], "tile", along(d, first)) for d in range(1, SIDE)
        ]

    def turn(parts, after):
        shape = (SIDE, 2) + parts[0].shape[1:]
        return pl.pallas_call(
            turn_kernel,
            in_specs=[vmem] * SIDE + [hbm] * len(after),
            out_specs=[vmem] * SIDE,
            out_shape=[jax.ShapeDtypeStruct(shape, bf16)] * SIDE,
            compiler_params=small,
            name="turn",
        )(*[x.reshape(shape) for x in parts], *[in_hbm(x) for x in after])

    def swap(parts, after):
        shape = (SIDE * SIDE,) + parts[0].shape[2:]
        crossing = pl.pallas_call(
            swap_kernel,
            in_specs=[vmem] * SIDE + [hbm] * len(after),
            out_specs=vmem,
            out_shape=jax.ShapeDtypeStruct(shape, bf16),
            compiler_params=small,
            name="swap",
        )(*parts, *[in_hbm(x) for x in after])
        return parts + [lax.ppermute(crossing, "tile", [(n, n ^ 1) for n in range(tiles)])]

    def exchange(sent, consume):
        arrived_a = lax.all_to_all(sent[0][0], "tile", split_axis=0, concat_axis=0, tiled=True)
        near_b = hop(sent[1], True)
        turned_b = turn(near_b, ())
        far_b = hop(turned_b, False)
        done_a = consume(0, [arrived_a])
        crossed_b = swap(far_b, done_a[:1])
        return [done_a, consume(1, crossed_b)]

    def spread(shares):
        moved = [
            lax.ppermute(x, "freq", [(z, (z + d + 1) % groups) for z in range(groups)])
            for d, x in enumerate(shares[1:])
        ]
        return [shares[0]] + moved

    starts = [sum(CHUNKS[:i]) for i in range(len(CHUNKS))]
    chunks = list(zip(starts, CHUNKS, ROUTES))
    sent = [coeff(*chunk) for chunk in chunks]
    back = exchange(sent, lambda n, arrived: resid(arrived, *chunks[n]))
    shares = exchange(back, lambda n, arrived: grad(arrived, *chunks[n][1:]))
    gathered = [x for share in shares for x in spread(share)]
    total = pl.pallas_call(
        functools.partial(finish_kernel, parts=groups),
        in_specs=[vmem] * len(gathered),
        out_specs=vmem,
        out_shape=jax.ShapeDtypeStruct((LAG_DEV, SOURCES, width), f32),
        compiler_params=params,
        name="finish",
    )(*gathered)
    return jnp.swapaxes(total, 1, 2)


def solution(mesh):
    placed = (
        P("freq", "tile", None),
        P("freq", "tile", None),
        P("freq", "tile", None, None, None, None),
        P("freq", "tile", None, None, None, None),
        P("freq", "tile", None),
        P("tile", None),
        P("freq"),
    )
    return jax.shard_map(
        per_device, mesh=mesh, in_specs=placed, out_specs=P("freq", "tile", None), check_vma=False
    )
```
